32 devices in a mesh: pipe: 2 (over x), row: 4 (over z), col: 4 (over y, core).
Axes of the slice: x: 2, y: 2, z: 4, core: 2. Of those that a mesh axis runs over, the one named last changes fastest.
Arguments:
- queries: bfloat16 [2, 64, 32, 4096], P('pipe', 'row', 'col'), may hold values from -6 to 6
- keys: bfloat16 [2, 64, 32, 4096], P('pipe', 'row', 'col'), may hold values from -6 to 6
- values: bfloat16 [2, 64, 32, 4096], P('pipe', 'row', 'col'), may hold values from -6 to 6
- cotangent: bfloat16 [64, 32, 4096], P('row', 'col'), may hold values from -6 to 6
Outputs:
- layer_out: bfloat16 [2, 64, 32, 4096], P('pipe', 'row', 'col')
- query_grad: bfloat16 [2, 64, 32, 4096], P('pipe', 'row', 'col')
- key_grad: bfloat16 [2, 64, 32, 4096], P('pipe', 'row', 'col')
- value_grad: bfloat16 [2, 64, 32, 4096], P('pipe', 'row', 'col')
The draws below stay inside these ranges and needn't reach their ends.
All inputs are finite; a program needn't handle non-finite values.
Results may differ from the reference program's by a relative error of at most 0.0095.
Values may be sent and summed in bfloat16 or wider, within the bound.
No kernel may reach another device: no remote copies, remote signals or barrier semaphores. Data moves between devices by JAX's collectives and lax.ppermute only.
A program may use at most 64 MiB of HBM per device.

```python
import math
import jax
import jax.numpy as jnp
from jax import lax

ROW_HEADS = 16
COL_HEADS = 16
HEAD_DIM = 128
LAYERS = 2
GRID_ROWS = 64
GRID_COLS = 32
WIDTH = 4096


def loud_draw(key, salt):
    full_shape = (LAYERS, GRID_ROWS, GRID_COLS, WIDTH)
    drawn = jax.random.truncated_normal(jax.random.fold_in(key, salt + 1), -6.0, 6.0, full_shape, jnp.float32)
    return drawn.astype(jnp.bfloat16)


def draw_queries(key, part):
    return loud_draw(key, 100)


def draw_keys(key, part):
    return loud_draw(key, 200)


def block_scale(key, dims, cuts, low, largest):
    def one(dim, blocks):
        draws = jax.random.uniform(jax.random.fold_in(jax.random.fold_in(key, 6), dim), (blocks,), jnp.float32, low / len(cuts), largest / len(cuts))
        return jnp.repeat(jnp.exp(draws), dims[dim] // blocks).reshape((-1,) + (1,) * (len(dims) - dim - 1))

    loudness = one(*cuts[0])
    for cut in cuts[1:]:
        loudness = loudness * one(*cut)
    return loudness


def noise(own_key, shape, deviation, reach, cuts=(), dtype=jnp.bfloat16):
    values = deviation * jax.random.normal(own_key, shape, jnp.float32)
    if cuts:
        values = values * block_scale(own_key, shape, cuts, -0.22, 0.18)
    return jnp.clip(values, -reach, reach).astype(dtype)


def setup_inputs(seed: int = 0) -> dict:
    streams_of = jax.random.split(jax.random.key(seed), 5)
    return {
        "queries": draw_queries(jax.random.fold_in(streams_of[4], 71), 0),
        "keys": draw_keys(jax.random.fold_in(streams_of[4], 71), 0),
        "values": noise(streams_of[2], (LAYERS, GRID_ROWS, GRID_COLS, WIDTH), 1.0, 6.0, ((0, 2), (1, 4), (2, 4))),
        "cotangent": noise(streams_of[3], (GRID_ROWS, GRID_COLS, WIDTH), 1.0, 6.0, ((0, 4), (1, 4))),
    }


masked_score = -1e+30

def lifted(array):
    return array.astype(jnp.float32)

def attention_forward(query_rows, key_rows, value_rows):
    head_scale = 1.0 / math.sqrt(HEAD_DIM)
    scores = jnp.einsum('blhd,bmhd->bhlm', lifted(query_rows), lifted(key_rows)) * head_scale
    length = scores.shape[-1]
    causal = jnp.arange(length)[:, None] >= jnp.arange(length)[None, :]
    scores = jnp.where(causal, scores, masked_score)
    row_max = lax.optimization_barrier(jnp.max(scores, axis=-1, keepdims=True))
    exponent = jnp.exp(scores - row_max)
    attn_weights = exponent / lax.optimization_barrier(jnp.sum(exponent, axis=-1, keepdims=True))
    rounded = attn_weights.astype(jnp.bfloat16)
    output = jnp.einsum('bhlm,bmhd->blhd', lifted(rounded), lifted(value_rows)).astype(jnp.bfloat16)
    return (output, attn_weights, rounded)

def forward_only(query_rows, key_rows, value_rows):
    return (attention_forward(query_rows, key_rows, value_rows)[0],)

def attention_backward(query_rows, key_rows, value_rows, grad_out):
    head_scale = 1.0 / math.sqrt(HEAD_DIM)
    recomputed = attention_forward(query_rows, key_rows, value_rows)
    attn_weights = recomputed[1]
    rounded = recomputed[2]
    grad_weights = jnp.einsum('blhd,bmhd->bhlm', lifted(grad_out), lifted(value_rows))
    row_delta = lax.optimization_barrier(jnp.sum(attn_weights * grad_weights, axis=-1, keepdims=True))
    grad_scores = (attn_weights * (grad_weights - row_delta)).astype(jnp.bfloat16)
    grad_query = (jnp.einsum('bhlm,bmhd->blhd', lifted(grad_scores), lifted(key_rows)) * head_scale).astype(jnp.bfloat16)
    grad_key = (jnp.einsum('bhlm,blhd->bmhd', lifted(grad_scores), lifted(query_rows)) * head_scale).astype(jnp.bfloat16)
    grad_value = jnp.einsum('bhlm,blhd->bmhd', lifted(rounded), lifted(grad_out)).astype(jnp.bfloat16)
    return (grad_query, grad_key, grad_value)

def blocked(function, arrays):
    batch_rows = arrays[0].shape[0]
    block_size = math.gcd(batch_rows, 8)
    folded = tuple((member.reshape((batch_rows // block_size, block_size) + member.shape[1:]) for member in arrays))
    results = lax.map(lambda pieces: function(*pieces), folded)
    return tuple((member.reshape((batch_rows,) + member.shape[2:]) for member in results))

def split_families(full):
    row_width = ROW_HEADS * HEAD_DIM
    rows_part = full[:, :, :row_width].reshape(GRID_ROWS, GRID_COLS, ROW_HEADS, HEAD_DIM)
    cols_part = full[:, :, row_width:].reshape(GRID_ROWS, GRID_COLS, COL_HEADS, HEAD_DIM)
    return (rows_part, jnp.transpose(cols_part, (1, 0, 2, 3)))

def join_families(rows_part, cols_part):
    rows_flat = rows_part.reshape(GRID_ROWS, GRID_COLS, ROW_HEADS * HEAD_DIM)
    cols_flat = jnp.transpose(cols_part, (1, 0, 2, 3)).reshape(GRID_ROWS, GRID_COLS, COL_HEADS * HEAD_DIM)
    return jnp.concatenate([rows_flat, cols_flat], axis=-1)

def layer_forward(queries_in, keys_in, values_in):
    query_parts = split_families(queries_in)
    key_parts = split_families(keys_in)
    value_parts = split_families(values_in)
    out_rows = blocked(forward_only, (query_parts[0], key_parts[0], value_parts[0]))[0]
    out_cols = blocked(forward_only, (query_parts[1], key_parts[1], value_parts[1]))[0]
    return join_families(out_rows, out_cols)

def layer_backward(queries_in, keys_in, values_in, grad_in):
    query_parts = split_families(queries_in)
    key_parts = split_families(keys_in)
    value_parts = split_families(values_in)
    grad_parts = split_families(grad_in)
    grads_rows = blocked(attention_backward, (query_parts[0], key_parts[0], value_parts[0], grad_parts[0]))
    grads_cols = blocked(attention_backward, (query_parts[1], key_parts[1], value_parts[1], grad_parts[1]))
    return tuple((join_families(grads_rows[index], grads_cols[index]) for index in range(3)))

def reference(queries, keys, values, cotangent):
    first_out = layer_forward(queries[0], keys[0], values[0])
    second_query = (lifted(queries[1]) + lifted(first_out)).astype(jnp.bfloat16)
    second_out = layer_forward(second_query, keys[1], values[1])
    second_grads = layer_backward(second_query, keys[1], values[1], cotangent)
    first_grads = layer_backward(queries[0], keys[0], values[0], second_grads[0])
    layer_out = jnp.stack([first_out, second_out])
    query_grad = jnp.stack([first_grads[0], second_grads[0]])
    key_grad = jnp.stack([first_grads[1], second_grads[1]])
    value_grad = jnp.stack([first_grads[2], second_grads[2]])
    return (layer_out, query_grad, key_grad, value_grad)
```

```python
import functools
import math

import jax
import jax.numpy as jnp
from jax import lax
from jax.experimental import pallas as pl
from jax.experimental.pallas import tpu as pltpu
from jax.sharding import PartitionSpec as P

ROW_HEADS = 16
HEAD_DIM = 128
TILE = 128


masked_score = -1e30
ANYWHERE = pl.BlockSpec(memory_space=pl.ANY)
ON_CHIP = pl.BlockSpec(memory_space=pltpu.VMEM)


def dot_nt(left, right):
    return lax.dot_general(left, right, (((1,), (1,)), ((), ())), preferred_element_type=jnp.float32)


def dot_nn(left, right):
    return lax.dot_general(left, right, (((1,), (0,)), ((), ())), preferred_element_type=jnp.float32)


def dot_tn(left, right):
    return lax.dot_general(left, right, (((0,), (0,)), ((), ())), preferred_element_type=jnp.float32)


def softmax_of(query, key, seen, scale):
    scores = jnp.where(seen, dot_nt(query, key) * scale, masked_score)
    exponent = jnp.exp(scores - jnp.max(scores, axis=-1, keepdims=True))
    weights = exponent / jnp.sum(exponent, axis=-1, keepdims=True)
    return weights, weights.astype(jnp.bfloat16)


def backward_of(query, key, value, grad, weights, rounded, scale):
    grad_weights = dot_nt(grad, value)
    delta = jnp.sum(weights * grad_weights, axis=-1, keepdims=True)
    grad_scores = (weights * (grad_weights - delta)).astype(jnp.bfloat16)
    return (
        dot_nn(grad_scores, key) * scale,
        dot_tn(grad_scores, query) * scale,
        dot_tn(rounded, grad),
    )


def both_layers(first, second, grad, seen, scale):
    bf16 = jnp.bfloat16
    query0, key0, value0 = first
    extra1, key1, value1 = second
    weights0, rounded0 = softmax_of(query0, key0, seen, scale)
    out0 = dot_nn(rounded0, value0)
    query1 = (extra1.astype(jnp.float32) + out0.astype(bf16).astype(jnp.float32)).astype(bf16)
    weights1, rounded1 = softmax_of(query1, key1, seen, scale)
    out1 = dot_nn(rounded1, value1)
    grads1 = backward_of(query1, key1, value1, grad, weights1, rounded1, scale)
    grads0 = backward_of(query0, key0, value0, grads1[0].astype(bf16), weights0, rounded0, scale)
    return ((out0,) + grads0, (out1,) + grads1)


class Family:
    def __init__(self, mesh, axis, base, width):
        self.axis = axis
        self.pipes = mesh.shape["pipe"]
        self.members = mesh.shape[axis]
        self.size = self.pipes * self.members
        self.base = base
        self.lanes = width // self.size

    def partner(self, step):
        pipe = lax.axis_index("pipe") ^ (step // self.members)
        place = lax.axis_index(self.axis) ^ (step % self.members)
        lanes = pl.ds(pl.multiple_of(self.base + (pipe * self.members + place) * self.lanes, TILE), self.lanes)
        return pipe, place, lanes

    def exchange(self, pieces):
        received = []
        for step in range(1, self.size):
            pairs = []
            for index in range(self.size):
                pipe, place = divmod(index, self.members)
                other = (pipe ^ (step // self.members)) * self.members + (place ^ (step % self.members))
                pairs.append((index, other))
            received.append(lax.ppermute(pieces[step - 1], ("pipe", self.axis), pairs))
        return received


def run_all(copies):
    for copy in copies:
        copy.start()
    for copy in copies:
        copy.wait()


def pack_kernel(family, *refs):
    queries, keys, values, cotangent = refs[:4]
    pieces, sems = refs[4:-1], refs[-1]
    copies = []
    for step in range(1, family.size):
        lanes = family.partner(step)[2]
        sources = [queries.at[0], keys.at[0], values.at[0]]
        if step < family.members:
            sources.append(cotangent)
        for place, source in enumerate(sources):
            copies.append(
                pltpu.make_async_copy(
                    source.at[:, :, lanes], pieces[step - 1].at[place], sems.at[len(copies)]
                )
            )
    run_all(copies)


def pack(family, queries, keys, values, cotangent):
    rows, cols = cotangent.shape[:2]
    shapes = [
        jax.ShapeDtypeStruct((4 if step < family.members else 3, rows, cols, family.lanes), jnp.bfloat16)
        for step in range(1, family.size)
    ]
    return pl.pallas_call(
        functools.partial(pack_kernel, family),
        out_shape=shapes,
        in_specs=[ANYWHERE] * 4,
        out_specs=[ON_CHIP] * len(shapes),
        scratch_shapes=[pltpu.SemaphoreType.DMA((4 * family.size,))],
        name="pack_" + family.axis,
    )(queries, keys, values, cotangent)


def bring_in(family, sources, pieces, tokens_in, grad_in, sems):
    queries, keys, values, cotangent = sources
    copies = []

    def add(source, target):
        copies.append(pltpu.make_async_copy(source, target, sems.at[len(copies)]))

    pipe, place, lanes = family.partner(0)
    for index, source in enumerate((queries, keys, values)):
        add(source.at[0, :, :, lanes], tokens_in.at[pipe, place, index])
    add(cotangent.at[:, :, lanes], grad_in.at[place])
    for step in range(1, family.size):
        pipe, place, _ = family.partner(step)
        piece = pieces[step - 1]
        if step < family.members:
            add(piece.at[pl.ds(0, 3)], tokens_in.at[pipe, place])
            add(piece.at[3], grad_in.at[place])
        else:
            add(piece, tokens_in.at[pipe, place])
    run_all(copies)


def send_out(family, results, outs, sems):
    copies = []
    for step in range(family.size):
        pipe, place, _ = family.partner(step)
        copies.append(pltpu.make_async_copy(results.at[pipe, place], outs[step], sems.at[step]))
    run_all(copies)


def rows_kernel(family, scale, *refs):
    n = family.size
    sources, pieces, outs = refs[:4], refs[4 : 3 + n], refs[3 + n : 3 + 2 * n]
    tokens_in, grad_in, results, sems = refs[3 + 2 * n :]
    bring_in(family, sources, pieces, tokens_in, grad_in, sems)
    members, _, rows, cols, lanes = tokens_in.shape[1:]
    span = max(1, TILE // (members * cols))
    size = members * span * cols
    part = span * cols

    def place_of(dim):
        token = lax.broadcasted_iota(jnp.int32, (size, size), dim)
        member, inner = token // part, token % part
        return inner // cols, member * cols + inner % cols

    query_row, query_col = place_of(0)
    key_row, key_col = place_of(1)
    seen = (query_row == key_row) & (key_col <= query_col)

    def step(index, carry):
        rows_here = pl.ds(index * span, span)
        for head in range(lanes // HEAD_DIM):
            here = slice(head * HEAD_DIM, (head + 1) * HEAD_DIM)

            def gather(view):
                parts = [
                    view(member, rows_here, here).astype(jnp.float32).reshape(part, HEAD_DIM)
                    for member in range(members)
                ]
                return jnp.concatenate(parts, axis=0).astype(jnp.bfloat16)

            layers = [
                [
                    gather(lambda m, r, c, layer=layer, i=i: tokens_in[layer, m, i, r, :, c])
                    for i in range(3)
                ]
                for layer in range(2)
            ]
            grad = gather(lambda m, r, c: grad_in[m, r, :, c])
            found = both_layers(layers[0], layers[1], grad, seen, scale)
            for layer in range(2):
                for i in range(4):
                    for member in range(members):
                        piece = found[layer][i][member * part : (member + 1) * part]
                        results[layer, member, i, rows_here, :, here] = piece.reshape(
                            span, cols, HEAD_DIM
                        ).astype(jnp.bfloat16)
        return carry

    lax.fori_loop(0, rows // span, step, 0)
    send_out(family, results, outs, sems)


def cols_kernel(family, scale, *refs):
    n = family.size
    sources, pieces, outs = refs[:4], refs[4 : 3 + n], refs[3 + n : 3 + 2 * n]
    tokens_in, grad_in, results, wide_in, wide_out, sems = refs[3 + 2 * n :]
    bring_in(family, sources, pieces, tokens_in, grad_in, sems)
    members, _, rows, cols, lanes = tokens_in.shape[1:]
    length = members * rows
    span = max(1, TILE // length)
    size = span * length

    def place_of(dim):
        token = lax.broadcasted_iota(jnp.int32, (size, size), dim)
        return token // length, token % length

    query_col, query_row = place_of(0)
    key_col, key_row = place_of(1)
    seen = (query_col == key_col) & (key_row <= query_row)
    per_member = rows * cols

    def one_head(head, carry):
        here = pl.ds(pl.multiple_of(head * HEAD_DIM, TILE), HEAD_DIM)
        for member in range(members):
            there = slice(member * per_member, (member + 1) * per_member)
            for layer in range(2):
                for i in range(3):
                    wide_in[layer * 3 + i, there, :] = (
                        tokens_in[layer, member, i, :, :, here]
                        .astype(jnp.float32)
                        .reshape(per_member, HEAD_DIM)
                    )
            wide_in[6, there, :] = (
                grad_in[member, :, :, here].astype(jnp.float32).reshape(per_member, HEAD_DIM)
            )
        for block in range(cols // span):

            def gather(index):
                parts = [
                    wide_in[index, pl.ds(block * span + k, length, stride=cols), :] for k in range(span)
                ]
                return jnp.concatenate(parts, axis=0).astype(jnp.bfloat16)

            arrays = [gather(index) for index in range(7)]
            found = both_layers(arrays[:3], arrays[3:6], arrays[6], seen, scale)
            for layer in range(2):
                for i in range(4):
                    for k in range(span):
                        wide_out[layer * 4 + i, pl.ds(block * span + k, length, stride=cols), :] = found[
                            layer
                        ][i][k * length : (k + 1) * length]
        for member in range(members):
            there = slice(member * per_member, (member + 1) * per_member)
            for layer in range(2):
                for i in range(4):
                    results[layer, member, i, :, :, here] = (
                        wide_out[layer * 4 + i, there, :]
                        .reshape(rows, cols, HEAD_DIM)
                        .astype(jnp.bfloat16)
                    )
        return carry

    lax.fori_loop(0, lanes // HEAD_DIM, one_head, 0)
    send_out(family, results, outs, sems)


def compute(family, body, wide, sources, pieces):
    rows, cols = sources[3].shape[:2]
    n, m, lanes = family.size, family.members, family.lanes
    scratch = [
        pltpu.VMEM((2, m, 3, rows, cols, lanes), jnp.bfloat16),
        pltpu.VMEM((m, rows, cols, lanes), jnp.bfloat16),
        pltpu.VMEM((2, m, 4, rows, cols, lanes), jnp.bfloat16),
    ]
    if wide:
        scratch += [
            pltpu.VMEM((7, m * rows * cols, HEAD_DIM), jnp.float32),
            pltpu.VMEM((8, m * rows * cols, HEAD_DIM), jnp.float32),
        ]
    scratch.append(pltpu.SemaphoreType.DMA((2 * n + 4,)))
    return pl.pallas_call(
        functools.partial(body, family, 1.0 / math.sqrt(HEAD_DIM)),
        out_shape=[jax.ShapeDtypeStruct((4, rows, cols, lanes), jnp.bfloat16)] * n,
        in_specs=[ANYWHERE] * 4 + [ON_CHIP] * (n - 1),
        out_specs=[ON_CHIP] * n,
        scratch_shapes=scratch,
        name="attend_" + family.axis,
    )(*sources, *pieces)


def unpack_kernel(families, *refs):
    count = sum(family.size for family in families)
    pieces, outs, sems = refs[:count], refs[count : count + 4], refs[-1]
    copies = []
    taken = 0
    for family in families:
        for step in range(family.size):
            lanes = family.partner(step)[2]
            for i in range(4):
                copies.append(
                    pltpu.make_async_copy(
                        pieces[taken].at[i], outs[i].at[0, :, :, lanes], sems.at[len(copies)]
                    )
                )
            taken += 1
    run_all(copies)


def unpack(families, pieces, shape):
    return pl.pallas_call(
        functools.partial(unpack_kernel, families),
        out_shape=[jax.ShapeDtypeStruct(shape, jnp.bfloat16)] * 4,
        in_specs=[ON_CHIP] * len(pieces),
        out_specs=[ANYWHERE] * 4,
        scratch_shapes=[pltpu.SemaphoreType.DMA((4 * len(pieces),))],
        name="unpack",
    )(*pieces)


def solution(mesh):
    def on_device(queries, keys, values, cotangent):
        row_width = ROW_HEADS * HEAD_DIM
        by_row = Family(mesh, "col", 0, row_width)
        by_col = Family(mesh, "row", row_width, cotangent.shape[-1] - row_width)
        sources = (queries, keys, values, cotangent)
        col_sent = by_col.exchange(pack(by_col, *sources))
        row_sent = by_row.exchange(pack(by_row, *sources))
        row_found = compute(by_row, rows_kernel, False, sources, row_sent)
        row_back = [row_found[0]] + by_row.exchange(row_found[1:])
        col_found = compute(by_col, cols_kernel, True, sources, col_sent)
        col_back = [col_found[0]] + by_col.exchange(col_found[1:])
        return tuple(unpack((by_row, by_col), row_back + col_back, queries.shape))

    native = P("pipe", "row", "col", None)
    return jax.shard_map(
        on_device,
        mesh=mesh,
        in_specs=(native, native, native, P("row", "col", None)),
        out_specs=(native,) * 4,
        check_vma=False,
    )
```
